32 devices in a mesh: dp: 4 (over z), expert: 8 (over y, x, core).
Axes of the slice: x: 2, y: 2, z: 4, core: 2. Of those that a mesh axis runs over, the one named last changes fastest.
Arguments:
- table_rows: bfloat16 [2048, 2048], P('expert'), may hold values from -4 to 4
- item_owner: int32 [8192, 3, 1], P(('dp', 'expert')), may hold values from 0 to 7; in each aligned block of 768 rows (0 to 767, 768 to 1535, ..., all dimensions but the last counted through in order) at most 192 rows name the same one
- item_row: int32 [8192, 3], P(('dp', 'expert')), may hold values from 0 to 255
- norm_gain: float32 [2048], replicated, may hold values from 0.1 to 1.9
- router: bfloat16 [2048, 16], replicated, may hold values from -0.125 to 0.125
- w_gate: bfloat16 [16, 2048, 768], P('expert'), may hold values from -0.125 to 0.125
- w_up: bfloat16 [16, 2048, 768], P('expert'), may hold values from -0.125 to 0.125
- w_down: bfloat16 [16, 2048, 768], P('expert'), may hold values from -0.21875 to 0.21875
- experts_of: int32 [8192, 2], P(('dp', 'expert')), may hold values from 0 to 15, all different within a row; in each aligned block of 256 rows (0 to 255, 256 to 511, ...) at most 64 rows name the same one
- grad_mixed: bfloat16 [8192, 2048], P(('dp', 'expert')), may hold values from -6 to 6
Outputs:
- mixed: bfloat16 [8192, 2048], P(('dp', 'expert'))
- grad_w_gate: bfloat16 [16, 2048, 768], P('expert', 'dp')
- grad_w_up: bfloat16 [16, 2048, 768], P('expert', 'dp')
- grad_w_down: bfloat16 [16, 2048, 768], P('expert', 'dp')
The draws below stay inside these ranges and needn't reach their ends.
Inputs may be any that keep to these rules, and one draw needn't show every extreme that they name: `item_owner`: within the 256 x 3 lookups of one device, at most 192 name rows of one owner; on some device some owner is named exactly 192 times. `experts_of`: each event names 2 different experts. Within the 256 events of one device at most 64 name one expert; on some device some expert is named exactly 64 times.
All inputs are finite; a program needn't handle non-finite values.
Results may differ from the reference program's by a relative error of at most 0.02.
Values may be sent and summed in bfloat16 or wider, within the bound.
A program may use at most 256 MiB of HBM per device.

```python
import math
import jax
import jax.numpy as jnp
import numpy as np
from jax import lax

D = 2048
FF = 768
TOP = 2
LEVELS = 3
TOK_DEV = 256
R_DEV = 256
OWNERS = 8
EXPERTS = 16
TOKENS = 8192
GROUP_TOK = 2048
CAP = 64
CAPF = 192
N_DP = 4


def plant(array, stream_key, low, largest):
    dims = array.shape
    spot = [jax.random.randint(jax.random.fold_in(stream_key, axis), (), 0, dims[axis]) for axis in range(len(dims))]
    array = array.at[tuple(spot)].set(low)
    longest = dims.index(max(dims))
    spot[longest] = (spot[longest] + 1) % dims[longest]
    return array.at[tuple(spot)].set(largest)


def block_levels(stream_key, shape, split, low, high):
    level = 1.0
    for dim, blocks in split:
        heights = jax.random.uniform(jax.random.fold_in(jax.random.fold_in(stream_key, 6), dim), (blocks,), jnp.float32, low / len(split), high / len(split))
        level = level * jnp.repeat(jnp.exp(heights), shape[dim] // blocks).reshape((-1,) + (1,) * (len(shape) - 1 - dim))
    return level


def shared_out(own_key, own, number, rows, number_of, top, bound, lean):
    ranking = jax.random.permutation(own_key, number_of)
    crowded, usual = load_shares(number_of, rows * top, bound, lean, True), load_shares(number_of, rows * top, bound, lean, False)
    places = jnp.arange(number_of)

    def named(lengths, turn):
        used = int((lengths > 0).sum())
        fixed = max(1, used // 4)
        passed = fixed + (places - fixed + turn * (used - fixed)) % max(1, number_of - fixed)
        return jnp.zeros((number_of,), jnp.int32).at[ranking[jnp.where(places < fixed, places, passed)]].set(jnp.asarray(lengths, jnp.int32))

    lengths = jnp.where(number % 4 == 0, named(crowded, number // 4), named(usual, number - number // 4 - 1))
    mixed = jax.random.permutation(jax.random.fold_in(own, 3), number_of)
    donor, receiver = mixed[0:number_of // 2 * 2:2], mixed[1:number_of // 2 * 2:2]
    room = jnp.minimum(lengths[donor] - 1, bound - lengths[receiver]) // 2
    room = jnp.where((donor == ranking[0]) | (receiver == ranking[0]) | (lengths[receiver] == 0), 0, jnp.maximum(room, 0))
    passed = jax.random.randint(jax.random.fold_in(own, 4), (number_of // 2,), 0, 1 << 20) % (room + 1)
    lengths = lengths.at[donor].add(-passed).at[receiver].add(passed)
    labels = jnp.searchsorted(jnp.cumsum(lengths), jnp.arange(rows * top), side="right").astype(jnp.int32)
    listing = labels.reshape(top, rows).T
    listing = listing[jax.random.permutation(jax.random.fold_in(own, 1), rows)]
    turn = jax.random.randint(jax.random.fold_in(own, 2), (rows, 1), 0, top)
    return jnp.take_along_axis(listing, (jnp.arange(top)[None, :] + turn) % top, axis=1)


def load_shares(count, total, reach, slope, full):
    portions = [(1 << 20) // math.isqrt(standing ** slope) + 1 for standing in range(1, count + 1)]
    largest = reach if full else min(reach, max(-(-total // count), total * portions[0] // sum(portions)))
    least = 1 if total - largest >= count - 1 else 0
    given, spare = [largest] + [least] * (count - 1), total - largest - least * (count - 1)
    while spare > 0:
        movable = [i for i in range(1, count) if given[i] < largest] or [i for i in range(1, count) if given[i] < reach]
        pool, budget = sum([portions[i] for i in movable]), spare
        for i in movable:
            extra = min(reach - given[i], max(1, budget * portions[i] // pool), spare)
            given[i] = given[i] + extra
            spare = spare - extra
    return np.array(given)


def normal_values(own_key, extent, deviation, bound, split=(), held_as=jnp.bfloat16):
    entries = deviation * jax.random.normal(own_key, extent, jnp.float32)
    if split:
        entries = entries * block_levels(own_key, extent, split, -0.22, 0.18)
    return jnp.clip(entries, -bound, bound).astype(held_as)


def setup_inputs(seed: int = 0) -> dict:
    seeds = jax.random.split(jax.random.key(seed), 11)
    table_rows = normal_values(seeds[0], (OWNERS * R_DEV, D), 0.6, 4.0, ((0, 8),))
    item_owner_keys = jax.random.split(jax.random.fold_in(seeds[1], 1), TOKENS * LEVELS // (TOK_DEV * LEVELS))
    item_owner_turns = jax.random.permutation(jax.random.fold_in(seeds[1], 3), TOKENS * LEVELS // (TOK_DEV * LEVELS))
    item_owner = jax.vmap(lambda own, number: shared_out(jax.random.fold_in(seeds[1], 2), own, number, TOK_DEV * LEVELS, OWNERS, 1, CAPF, 2))(item_owner_keys, item_owner_turns).reshape((TOKENS, LEVELS, 1))
    item_row = plant(jax.random.randint(seeds[2], (TOKENS, LEVELS), 0, R_DEV), jax.random.fold_in(seeds[2], 1), 0, R_DEV - 1).astype(jnp.int32)
    norm_gain = jnp.clip(1.0 + 0.18 * jax.random.normal(seeds[3], (D,), jnp.float32), 0.1, 1.9)
    router = normal_values(seeds[4], (D, EXPERTS), D ** -0.5, 0.125)
    w_gate = normal_values(seeds[5], (EXPERTS, D, FF), D ** -0.5, 0.125, ((0, 8),))
    w_up = normal_values(seeds[6], (EXPERTS, D, FF), D ** -0.5, 0.125, ((0, 8),))
    w_down = normal_values(seeds[7], (EXPERTS, D, FF), FF ** -0.5, 0.21875, ((0, 8),))
    experts_of_keys = jax.random.split(jax.random.fold_in(seeds[8], 1), TOKENS // TOK_DEV)
    experts_of_turns = jax.random.permutation(jax.random.fold_in(seeds[8], 3), TOKENS // TOK_DEV)
    experts_of = jax.vmap(lambda own, number: shared_out(jax.random.fold_in(seeds[8], 2), own, number, TOK_DEV, EXPERTS, TOP, CAP, 2))(experts_of_keys, experts_of_turns).reshape((TOKENS, TOP))
    grad_mixed = normal_values(seeds[9], (TOKENS, D), 1.0, 6.0, ((0, 32),))
    return {"table_rows": table_rows, "item_owner": item_owner, "item_row": item_row, "norm_gain": norm_gain, "router": router, "w_gate": w_gate, "w_up": w_up, "w_down": w_down, "experts_of": experts_of, "grad_mixed": grad_mixed}


def reference(table_rows, item_owner, item_row, norm_gain, router, w_gate, w_up, w_down, experts_of, grad_mixed):
    rows = (item_owner[:, :, 0] * R_DEV + item_row).astype(jnp.int32)
    summed = jnp.zeros((TOKENS, D), jnp.float32)
    for level in range(LEVELS):
        summed = summed + table_rows[rows[:, level]].astype(jnp.float32)
    embedded = summed.astype(jnp.bfloat16)
    base = lax.optimization_barrier(embedded).astype(jnp.float32)
    normed = (base * lax.rsqrt(lax.optimization_barrier(jnp.mean(base * base, axis=-1, keepdims=True)) + 1e-05) * norm_gain).astype(jnp.bfloat16)
    scores = jax.nn.sigmoid(jnp.dot(normed, router, preferred_element_type=jnp.float32))
    picked = jnp.take_along_axis(scores, experts_of, axis=1)
    weight = picked / lax.optimization_barrier(jnp.sum(picked, axis=1, keepdims=True))
    scaled = (weight[:, :, None] * grad_mixed.astype(jnp.float32)[:, None, :]).astype(jnp.bfloat16)
    pairs = TOKENS * TOP
    scaled_flat = scaled.reshape(pairs, D)
    weight_flat = weight.reshape(pairs)
    pair_ids = jnp.arange(pairs, dtype=jnp.int32)
    group = pair_ids // TOP // GROUP_TOK
    keys = (experts_of.reshape(pairs) * N_DP + group).astype(jnp.int32)
    order = jnp.argsort(keys, stable=True).astype(jnp.int32)
    counts = jax.ops.segment_sum(jnp.ones((pairs,), jnp.int32), keys, num_segments=EXPERTS * N_DP).astype(jnp.int32)
    starts = (jnp.cumsum(counts) - counts).astype(jnp.int32)
    block = OWNERS * CAP
    order_pad = jnp.concatenate([order, jnp.zeros((block,), jnp.int32)])
    positions = jnp.arange(block, dtype=jnp.int32)
    high = lax.Precision.HIGHEST

    def per_expert(acc, items):
        wg, wu, wd, expert = items
        wgf = wg.astype(jnp.float32)
        wuf = wu.astype(jnp.float32)
        wdf = wd.astype(jnp.float32)
        totals = [jnp.zeros((D, FF), jnp.float32) for _ in range(3)]
        for group_id in range(N_DP):
            slot_key = expert * N_DP + group_id
            index = lax.dynamic_slice(order_pad, (starts[slot_key].astype(jnp.int32),), (block,))
            valid = (positions < counts[slot_key]).astype(jnp.float32)[:, None]
            token = index // TOP
            rows_in = normed[token].astype(jnp.float32) * valid
            grads_in = scaled_flat[index].astype(jnp.float32) * valid
            gate = jnp.dot(rows_in, wgf, precision=high)
            up = jnp.dot(rows_in, wuf, precision=high)
            hidden = (jax.nn.silu(gate) * up).astype(jnp.bfloat16)
            hidden_f = lax.optimization_barrier(hidden).astype(jnp.float32)
            produced = jnp.dot(hidden_f, wdf.T, precision=high).astype(jnp.bfloat16)
            produced_f = lax.optimization_barrier(produced).astype(jnp.float32)
            acc = acc.at[token].add(weight_flat[index][:, None] * valid * produced_f)
            grad_hidden = jnp.dot(grads_in, wdf, precision=high)
            sig = jax.nn.sigmoid(gate)
            grad_gate = (grad_hidden * up * sig * (1.0 + gate * (1.0 - sig))).astype(jnp.bfloat16)
            grad_up = (grad_hidden * gate * sig).astype(jnp.bfloat16)
            part_gate = jnp.dot(rows_in.T, lax.optimization_barrier(grad_gate).astype(jnp.float32), precision=high)
            part_up = jnp.dot(rows_in.T, lax.optimization_barrier(grad_up).astype(jnp.float32), precision=high)
            part_down = jnp.dot(grads_in.T, hidden_f, precision=high)
            parts = [part_gate, part_up, part_down]
            for which in range(3):
                rounded = lax.optimization_barrier(parts[which].astype(jnp.bfloat16))
                totals[which] = totals[which] + rounded.astype(jnp.float32)
        return (acc, (totals[0].astype(jnp.bfloat16), totals[1].astype(jnp.bfloat16), totals[2].astype(jnp.bfloat16)))
    acc, grads = lax.scan(per_expert, jnp.zeros((TOKENS, D), jnp.float32), (w_gate, w_up, w_down, jnp.arange(EXPERTS, dtype=jnp.int32)))
    mixed = (base + acc).astype(jnp.bfloat16)
    return (mixed, grads[0], grads[1], grads[2])
```

```python
import jax
import jax.numpy as jnp
from jax import lax
from jax.sharding import PartitionSpec as P

BF = jnp.bfloat16
F32 = jnp.float32


def multi_hot(rows, keep, row_count):
    ids = jnp.arange(row_count, dtype=jnp.int32)
    total = 0.0
    for level in range(rows.shape[-1]):
        total = total + (ids == rows[..., level : level + 1]).astype(F32)
    if keep is not None:
        total = jnp.where(keep[..., None], total, 0.0)
    return total.astype(BF)


def normalize(embedded, gain):
    base = embedded.astype(F32)
    return base, (
        base * lax.rsqrt(jnp.mean(base * base, axis=-1, keepdims=True) + 1e-05) * gain
    ).astype(BF)


def pick(scores, ids):
    experts = jnp.arange(scores.shape[-1], dtype=jnp.int32)
    return jnp.sum(jnp.where(experts == ids[..., None], scores, 0.0), axis=-1)


def per_device(
    table_rows,
    item_owner,
    item_row,
    norm_gain,
    router,
    w_gate,
    w_up,
    w_down,
    experts_of,
    grad_mixed,
):
    owners = lax.axis_size("expert")
    groups = lax.axis_size("dp")
    me = lax.axis_index("expert")
    mine = lax.axis_index("dp")
    tok, levels = item_row.shape
    rows_own, width = table_rows.shape
    experts = router.shape[1]
    local = w_gate.shape[0]
    ff = w_gate.shape[2]
    top = experts_of.shape[1]
    cap = 2 * tok * top // experts
    part = width // groups
    rows_all = owners * rows_own

    fields = jnp.concatenate([item_owner[:, :, 0].T, item_row.T, experts_of.T], axis=0)
    meta = lax.all_gather(fields, ("dp", "expert"), axis=0, tiled=False)
    table = lax.all_gather(table_rows, "expert", axis=0, tiled=True)

    chosen = experts_of.T
    each = jnp.arange(experts, dtype=jnp.int32)
    own_k = each[None, :, None] == chosen[:, None, :]
    own_match = jnp.any(own_k, axis=0)
    own_pos = jnp.cumsum(own_match.astype(jnp.int32), axis=1) - 1
    places = jnp.arange(cap, dtype=jnp.int32)
    own_at = own_pos[:, None, :] == places[None, :, None]
    own_hot = (own_at & own_match[:, None, :]).astype(BF)
    send = jnp.einsum("ect,td->ecd", own_hot, grad_mixed, preferred_element_type=F32).astype(BF)
    arrived = lax.all_to_all(
        send.reshape(owners, local, cap, width), "expert", split_axis=0, concat_axis=0, tiled=True
    )

    sliced = grad_mixed.reshape(tok, groups, part).transpose(1, 0, 2)
    sliced = lax.all_to_all(sliced, "dp", split_axis=0, concat_axis=0, tiled=True)
    sliced = jnp.roll(sliced, -mine, axis=0)
    slices = lax.all_gather(sliced, "expert", axis=0, tiled=False)

    meta = jnp.roll(meta.reshape(groups, owners, -1, tok), -mine, axis=0)
    here = me * local + jnp.arange(local, dtype=jnp.int32)
    match = jnp.any(
        meta[None, :, :, 2 * levels :, :] == here[:, None, None, None, None], axis=3
    )
    count = jnp.cumsum(match.astype(jnp.int32), axis=-1)
    hot = (
        ((count - 1)[:, :, :, None, :] == places[:, None]) & match[:, :, :, None, :]
    ).astype(BF)
    keep = places < count[..., -1:]
    slot_meta = jnp.einsum(
        "egbct,gbft->egbcf", hot, meta.astype(BF), preferred_element_type=F32
    ).astype(jnp.int32)
    slot_rows = slot_meta[..., :levels] * rows_own + slot_meta[..., levels : 2 * levels]
    slot_experts = slot_meta[..., 2 * levels :]

    def flat(x, first, last):
        x = x[:, first:last]
        return x.reshape((local, (last - first) * owners * cap) + x.shape[4:])

    def forward(first, last):
        spread = multi_hot(flat(slot_rows, first, last), flat(keep, first, last), rows_all)
        embedded = jnp.einsum("esr,rd->esd", spread, table, preferred_element_type=F32).astype(BF)
        _, normed = normalize(embedded, norm_gain)
        scores = jax.nn.sigmoid(
            jnp.einsum("esd,dx->esx", normed, router, preferred_element_type=F32)
        )
        ids = flat(slot_experts, first, last)
        total = sum(pick(scores, ids[..., k]) for k in range(top))
        weight = pick(scores, jnp.broadcast_to(here[:, None], scores.shape[:2])) / total
        gate = jnp.einsum("esd,edf->esf", normed, w_gate, preferred_element_type=F32)
        up = jnp.einsum("esd,edf->esf", normed, w_up, preferred_element_type=F32)
        hidden = (jax.nn.silu(gate) * up).astype(BF)
        columns = lax.dynamic_slice_in_dim(normed, mine * part, part, axis=2)
        return weight, gate, up, hidden, columns

    def grads(gate, up, grad_hidden):
        sig = jax.nn.sigmoid(gate)
        grad_gate = (grad_hidden * up * sig * (1.0 + gate * (1.0 - sig))).astype(BF)
        grad_up = (grad_hidden * gate * sig).astype(BF)
        return grad_gate, grad_up

    def scaled_columns(weight, first, last):
        taken = jnp.einsum(
            "egbct,bgtd->egbcd",
            hot[:, first:last],
            slices[:, first:last],
            preferred_element_type=F32,
        )
        return (weight[:, :, None] * taken.reshape(weight.shape + (part,))).astype(BF)

    def outer(a, b):
        return jnp.einsum("esd,esf->edf", a, b, preferred_element_type=F32)

    weight, gate, up, hidden, columns = forward(0, 1)
    arrived = arrived.transpose(1, 0, 2, 3).reshape(local, owners * cap, width)
    scaled = (weight[:, :, None] * arrived.astype(F32)).astype(BF)
    grad_hidden = jnp.einsum("esd,edf->esf", scaled, w_down, preferred_element_type=F32)
    grad_hidden_all = lax.all_gather(grad_hidden.astype(BF), "dp", axis=0, tiled=False)
    produced = jnp.einsum("esf,edf->esd", hidden, w_down, preferred_element_type=F32).astype(BF)
    produced = produced.reshape(local, owners, cap, width).transpose(1, 0, 2, 3)
    returned = lax.all_to_all(produced, "expert", split_axis=0, concat_axis=0, tiled=True)

    weight_o, gate_o, up_o, hidden_o, columns_o = forward(1, groups)
    grad_hidden_o = jnp.concatenate(
        [
            lax.dynamic_index_in_dim(
                grad_hidden_all, lax.rem(mine + i, groups), axis=0, keepdims=False
            )
            for i in range(1, groups)
        ],
        axis=1,
    ).astype(F32)
    grad_gate, grad_up = grads(gate, up, grad_hidden)
    grad_gate_o, grad_up_o = grads(gate_o, up_o, grad_hidden_o)
    out_gate = outer(columns, grad_gate) + outer(columns_o, grad_gate_o)
    out_up = outer(columns, grad_up) + outer(columns_o, grad_up_o)
    scaled_c = scaled_columns(weight, 0, 1)
    scaled_o = scaled_columns(weight_o, 1, groups)
    out_down = outer(scaled_c, hidden) + outer(scaled_o, hidden_o)

    own_rows = item_owner[:, :, 0] * rows_own + item_row
    embedded = jnp.dot(
        multi_hot(own_rows, None, rows_all), table, preferred_element_type=F32
    ).astype(BF)
    base, normed = normalize(embedded, norm_gain)
    scores = jax.nn.sigmoid(jnp.dot(normed, router, preferred_element_type=F32))
    picked = [pick(scores, experts_of[:, k]) for k in range(top)]
    total = sum(picked)
    mixed = base
    for k in range(top):
        back = (own_at & own_k[k][:, None, :]).astype(BF)
        rows = jnp.einsum(
            "ect,ecd->td",
            back,
            returned.reshape(experts, cap, width),
            preferred_element_type=F32,
        )
        mixed = mixed + (picked[k] / total)[:, None] * rows
    return mixed.astype(BF), out_gate.astype(BF), out_up.astype(BF), out_down.astype(BF)


def solution(mesh):
    placed = (
        P("expert", None),
        P(("dp", "expert"), None, None),
        P(("dp", "expert"), None),
        P(),
        P(),
        P("expert", None, None),
        P("expert", None, None),
        P("expert", None, None),
        P(("dp", "expert"), None),
        P(("dp", "expert"), None),
    )
    return jax.shard_map(
        per_device,
        mesh=mesh,
        in_specs=placed,
        out_specs=(
            P(("dp", "expert"), None),
            P("expert", "dp", None),
            P("expert", "dp", None),
            P("expert", "dp", None),
        ),
        check_vma=False,
    )
```

```python
import jax
import jax.numpy as jnp
from jax import lax
from jax.sharding import PartitionSpec as P

BF = jnp.bfloat16
F32 = jnp.float32


def multi_hot(rows, keep, row_count):
    ids = jnp.arange(row_count, dtype=jnp.int32)
    total = 0.0
    for level in range(rows.shape[-1]):
        total = total + (ids == rows[..., level : level + 1]).astype(F32)
    if keep is not None:
        total = jnp.where(keep[..., None], total, 0.0)
    return total.astype(BF)


def normalize(embedded, gain):
    base = embedded.astype(F32)
    return base, (
        base * lax.rsqrt(jnp.mean(base * base, axis=-1, keepdims=True) + 1e-05) * gain
    ).astype(BF)


def pick(scores, ids):
    experts = jnp.arange(scores.shape[-1], dtype=jnp.int32)
    return jnp.sum(jnp.where(experts == ids[..., None], scores, 0.0), axis=-1)


def per_device(
    table_rows,
    item_owner,
    item_row,
    norm_gain,
    router,
    w_gate,
    w_up,
    w_down,
    experts_of,
    grad_mixed,
):
    owners = lax.axis_size("expert")
    groups = lax.axis_size("dp")
    me = lax.axis_index("expert")
    mine = lax.axis_index("dp")
    tok, levels = item_row.shape
    rows_own, width = table_rows.shape
    experts = router.shape[1]
    local = w_gate.shape[0]
    top = experts_of.shape[1]
    cap = 2 * tok * top // experts
    part = width // groups
    rows_all = owners * rows_own

    fields = jnp.concatenate([item_owner[:, :, 0].T, item_row.T, experts_of.T], axis=0)
    meta = lax.all_gather(fields, ("dp", "expert"), axis=0, tiled=False)
    table_rows, grad_mixed, meta = lax.optimization_barrier((table_rows, grad_mixed, meta))
    table = lax.all_gather(table_rows, "expert", axis=0, tiled=True)
    meta = meta.reshape(groups, owners, -1, tok)
    places = jnp.arange(cap, dtype=jnp.int32)

    chosen = experts_of.T
    each = jnp.arange(experts, dtype=jnp.int32)
    own_k = each[None, :, None] == chosen[:, None, :]
    own_match = jnp.any(own_k, axis=0)
    own_pos = jnp.cumsum(own_match.astype(jnp.int32), axis=1) - 1
    own_at = own_pos[:, None, :] == places[None, :, None]
    own_hot = (own_at & own_match[:, None, :]).astype(BF)
    send = jnp.einsum("ect,td->ecd", own_hot, grad_mixed, preferred_element_type=F32).astype(BF)
    arrived = lax.all_to_all(
        send.reshape(owners, local, cap, width), "expert", split_axis=0, concat_axis=0, tiled=True
    )

    grad_mixed, arrived = lax.optimization_barrier((grad_mixed, arrived))
    sliced = grad_mixed.reshape(tok, groups, part).transpose(1, 0, 2)
    sliced = lax.all_to_all(sliced, "dp", split_axis=0, concat_axis=0, tiled=True)

    rolled = jnp.roll(meta, -mine, axis=0)
    here = me * local + jnp.arange(local, dtype=jnp.int32)
    match = jnp.any(
        rolled[None, :, :, 2 * levels :, :] == here[:, None, None, None, None], axis=3
    )
    count = jnp.cumsum(match.astype(jnp.int32), axis=-1)
    hot = (
        ((count - 1)[:, :, :, None, :] == places[:, None]) & match[:, :, :, None, :]
    ).astype(BF)
    keep = places < count[..., -1:]
    slot_meta = jnp.einsum(
        "egbct,gbft->egbcf", hot, rolled.astype(BF), preferred_element_type=F32
    ).astype(jnp.int32)
    slot_rows = slot_meta[..., :levels] * rows_own + slot_meta[..., levels : 2 * levels]
    slot_experts = slot_meta[..., 2 * levels :]

    def flat(x, first, last):
        x = x[first:last]
        return x.reshape(((last - first) * owners * cap,) + x.shape[3:])

    def forward(e, rows, kept, ids):
        spread = multi_hot(rows, kept, rows_all)
        embedded = jnp.dot(spread, table, preferred_element_type=F32).astype(BF)
        _, normed = normalize(embedded, norm_gain)
        scores = jax.nn.sigmoid(jnp.dot(normed, router, preferred_element_type=F32))
        total = sum(pick(scores, ids[..., k]) for k in range(top))
        weight = pick(scores, jnp.broadcast_to(here[e], scores.shape[:1])) / total
        gate = jnp.dot(normed, w_gate[e], preferred_element_type=F32)
        up = jnp.dot(normed, w_up[e], preferred_element_type=F32)
        hidden = (jax.nn.silu(gate) * up).astype(BF)
        columns = lax.dynamic_slice_in_dim(normed, mine * part, part, axis=1)
        return weight, gate, up, hidden, columns

    def grads(gate, up, grad_hidden):
        sig = jax.nn.sigmoid(gate)
        grad_gate = (grad_hidden * up * sig * (1.0 + gate * (1.0 - sig))).astype(BF)
        grad_up = (grad_hidden * gate * sig).astype(BF)
        return grad_gate, grad_up

    def outer(a, b):
        return lax.dot_general(a, b, (((0,), (0,)), ((), ())), preferred_element_type=F32)

    own, travelling, everywhere = [], [], []
    for e in range(local):
        weight, gate, up, hidden, columns = forward(
            e, flat(slot_rows[e], 0, 1), flat(keep[e], 0, 1), flat(slot_experts[e], 0, 1)
        )
        scaled = (weight[:, None] * arrived[:, e].reshape(owners * cap, width).astype(F32)).astype(BF)
        grad_hidden = jnp.einsum("sd,df->sf", scaled, w_down[e], preferred_element_type=F32)
        leaving = grad_hidden.astype(BF)
        everywhere.append(lax.all_gather(leaving, "dp", axis=0, tiled=False))
        travelling.append(leaving)
        own.append((weight, gate, up, hidden, columns, grad_hidden))

    travelling, own, slot_rows, own_rows, column_of = lax.optimization_barrier(
        (travelling, own, slot_rows, item_owner[:, :, 0] * rows_own + item_row, meta)
    )
    produced = jnp.stack(
        [
            jnp.dot(own[e][3], w_down[e].T, preferred_element_type=F32)
            .astype(BF)
            .reshape(owners, cap, width)
            for e in range(local)
        ],
        axis=1,
    )
    returned = lax.all_to_all(produced, "expert", split_axis=0, concat_axis=0, tiled=True)

    column = lax.dynamic_index_in_dim(column_of, me, axis=1, keepdims=False)[:, 2 * levels :, :]
    column = jnp.any(each[None, :, None, None] == column[:, None, :, :], axis=2)
    column_pos = jnp.cumsum(column.astype(jnp.int32), axis=-1) - 1
    column_hot = (
        (column_pos[:, :, None, :] == places[:, None]) & column[:, :, None, :]
    ).astype(BF)
    out_slices = jnp.einsum(
        "gsct,gtd->sgcd", column_hot, sliced, preferred_element_type=F32
    ).astype(BF)
    slices = lax.all_to_all(
        out_slices.reshape(owners, local, groups, cap, part),
        "expert",
        split_axis=0,
        concat_axis=0,
        tiled=True,
    )

    order = [lax.rem(mine + i, groups) for i in range(groups)]
    ready, out_down = [], []
    for e in range(local):
        weight, gate, up, hidden, columns, grad_hidden = own[e]
        weight_o, gate_o, up_o, hidden_o, columns_o = forward(
            e,
            flat(slot_rows[e], 1, groups),
            flat(keep[e], 1, groups),
            flat(slot_experts[e], 1, groups),
        )
        grad_gate, grad_up = grads(gate, up, grad_hidden)
        ready.append((outer(columns, grad_gate), outer(columns, grad_up), gate_o, up_o, columns_o))
        mine_slices = jnp.concatenate(
            [
                lax.dynamic_index_in_dim(slices[:, e], i, axis=1, keepdims=False).reshape(
                    owners * cap, part
                )
                for i in order
            ],
            axis=0,
        )
        weight_all = jnp.concatenate([weight, weight_o], axis=0)
        scaled_all = (weight_all[:, None] * mine_slices.astype(F32)).astype(BF)
        out_down.append(outer(scaled_all, jnp.concatenate([hidden, hidden_o], axis=0)))
    out_gate, out_up = [], []
    for e in range(local):
        own_gate, own_up, gate_o, up_o, columns_o = ready[e]
        grad_hidden_o = jnp.concatenate(
            [
                lax.dynamic_index_in_dim(everywhere[e], i, axis=0, keepdims=False)
                for i in order[1:]
            ],
            axis=0,
        ).astype(F32)
        grad_gate_o, grad_up_o = grads(gate_o, up_o, grad_hidden_o)
        gate_e = (own_gate + outer(columns_o, grad_gate_o)).astype(BF)
        up_e = (own_up + outer(columns_o, grad_up_o)).astype(BF)
        if e + 1 < local:
            gate_e, up_e, everywhere[e + 1] = lax.optimization_barrier(
                (gate_e, up_e, everywhere[e + 1])
            )
        out_gate.append(gate_e)
        out_up.append(up_e)
    out_down = [x.astype(BF) for x in out_down]
    out_gate, out_up, out_down = [jnp.stack(x) for x in (out_gate, out_up, out_down)]

    embedded = jnp.dot(
        multi_hot(own_rows, None, rows_all), table, preferred_element_type=F32
    ).astype(BF)
    base, normed = normalize(embedded, norm_gain)
    scores = jax.nn.sigmoid(jnp.dot(normed, router, preferred_element_type=F32))
    picked = [pick(scores, experts_of[:, k]) for k in range(top)]
    total = sum(picked)
    mixed = base
    for k in range(top):
        back = (own_at & own_k[k][:, None, :]).astype(BF)
        rows = jnp.einsum(
            "ect,ecd->td",
            back,
            returned.reshape(experts, cap, width),
            preferred_element_type=F32,
        )
        mixed = mixed + (picked[k] / total)[:, None] * rows
    return mixed.astype(BF), out_gate, out_up, out_down


def solution(mesh):
    placed = (
        P("expert", None),
        P(("dp", "expert"), None, None),
        P(("dp", "expert"), None),
        P(),
        P(),
        P("expert", None, None),
        P("expert", None, None),
        P("expert", None, None),
        P(("dp", "expert"), None),
        P(("dp", "expert"), None),
    )
    return jax.shard_map(
        per_device,
        mesh=mesh,
        in_specs=placed,
        out_specs=(
            P(("dp", "expert"), None),
            P("expert", "dp", None),
            P("expert", "dp", None),
            P("expert", "dp", None),
        ),
        check_vma=False,
    )
```
